32 devices in a mesh: dp: 16 (over z, x, core), tensor: 2 (over y).
Axes of the slice: x: 2, y: 2, z: 4, core: 2. Of those that a mesh axis runs over, the one named last changes fastest.
Arguments:
- inputs: bfloat16 [4096, 768], P('dp'), may hold values from -6 to 6
- encoded: bfloat16 [4096, 768], P('dp'), may hold values from -6 to 6
- cotangent: bfloat16 [4096, 768], P('dp'), may hold values from -6 to 6
- buckets: int32 [256, 256], replicated, may hold values from 0 to 31
- gain_self: float32 [768], replicated, may hold values from 0.5 to 1.5
- gain_cross: float32 [768], replicated, may hold values from 0.5 to 1.5
- gain_ffn: float32 [768], replicated, may hold values from 0.5 to 1.5
- bias_table: float32 [32, 12], P(None, 'tensor'), may hold values from -4 to 4
- self_query: bfloat16 [768, 768], P(None, 'tensor'), may hold values from -0.0546875 to 0.0546875
- self_attention_key: bfloat16 [768, 768], P(None, 'tensor'), may hold values from -0.21875 to 0.21875
- self_value: bfloat16 [768, 768], P(None, 'tensor'), may hold values from -0.21875 to 0.21875
- self_out: bfloat16 [768, 768], P('tensor'), may hold values from -0.625 to 0.625
- cross_query: bfloat16 [768, 768], P(None, 'tensor'), may hold values from -0.0546875 to 0.0546875
- cross_key: bfloat16 [768, 768], P(None, 'tensor'), may hold values from -0.21875 to 0.21875
- cross_value: bfloat16 [768, 768], P(None, 'tensor'), may hold values from -0.21875 to 0.21875
- cross_out: bfloat16 [768, 768], P('tensor'), may hold values from -0.625 to 0.625
- ffn_gate: bfloat16 [768, 2048], P(None, 'tensor'), may hold values from -0.21875 to 0.21875
- ffn_up: bfloat16 [768, 2048], P(None, 'tensor'), may hold values from -0.21875 to 0.21875
- ffn_down: bfloat16 [2048, 768], P('tensor'), may hold values from -0.125 to 0.125
Outputs:
- output: bfloat16 [4096, 768], P(('dp', 'tensor'))
- input_grad: float32 [4096, 768], P(('dp', 'tensor'))
- encoder_states_gradient: float32 [4096, 768], P(('dp', 'tensor'))
- gain_self_grad: float32 [768], replicated
- gain_cross_grad: float32 [768], replicated
- gain_ffn_grad: float32 [768], replicated
- bias_table_grad: float32 [32, 12], P(None, 'tensor')
- self_query_grad: float32 [768, 768], P('dp', 'tensor')
- self_key_grad: float32 [768, 768], P('dp', 'tensor')
- self_value_grad: float32 [768, 768], P('dp', 'tensor')
- self_out_grad: float32 [768, 768], P('tensor', 'dp')
- cross_query_grad: float32 [768, 768], P('dp', 'tensor')
- cross_key_grad: float32 [768, 768], P('dp', 'tensor')
- cross_value_grad: float32 [768, 768], P('dp', 'tensor')
- cross_out_grad: float32 [768, 768], P('tensor', 'dp')
- ffn_gate_grad: float32 [768, 2048], P('dp', 'tensor')
- ffn_up_grad: float32 [768, 2048], P('dp', 'tensor')
- ffn_down_grad: float32 [2048, 768], P('tensor', 'dp')
The draws below stay inside these ranges and needn't reach their ends.
All inputs are finite; a program needn't handle non-finite values.
Results may differ from the reference program's by a relative error of at most 0.035.
Values may be sent and summed in bfloat16 or wider, within the bound.
No kernel may reach another device: no remote copies, remote signals or barrier semaphores. Data moves between devices by JAX's collectives and lax.ppermute only.
A program may use at most 128 MiB of HBM per device.

```python
import jax
import jax.numpy as jnp
from jax import lax

D = 768
H = 12
HD = 64
FF = 2048
BUCKETS = 32
LEN = 256
ENC = 256
TOKENS = 4096
ENC_TOKENS = 4096


def touch_ends(drawn, stream_key, low, top_value):
    place = [jax.random.randint(jax.random.fold_in(stream_key, axis), (), 0, length) for axis, length in enumerate(drawn.shape)]
    widest = drawn.shape.index(max(drawn.shape))
    beside = place[:widest] + [(place[widest] + 1) % drawn.shape[widest]] + place[widest + 1:]
    return drawn.at[tuple(place)].set(low).at[tuple(beside)].set(top_value)


def level_of(key, dims, split, low, high):
    factor_of = 1.0
    for axis_at, blocks in split:
        draws = jax.random.uniform(jax.random.fold_in(jax.random.fold_in(key, 6), axis_at), (blocks,), jnp.float32, low / len(split), high / len(split))
        factor_of = factor_of * jnp.repeat(jnp.exp(draws), dims[axis_at] // blocks).reshape((-1,) + (1,) * (len(dims) - 1 - axis_at))
    return factor_of


def scatter_about(rng, shape, deviation, reach, shards=(), kind=jnp.bfloat16):
    values = jax.random.normal(rng, shape, jnp.float32) * deviation
    if len(shards) > 0:
        values = level_of(rng, shape, shards, -0.22, 0.18) * values
    return jnp.clip(values, min=-reach, max=reach).astype(kind)


def setup_inputs(seed: int = 0) -> dict:
    key_list = jax.random.split(jax.random.key(seed), 20)
    return {
        "inputs": scatter_about(key_list[0], (TOKENS, D), 1.0, 6.0, ((0, 16),)),
        "encoded": scatter_about(key_list[1], (ENC_TOKENS, D), 1.0, 6.0, ((0, 16),)),
        "cotangent": scatter_about(key_list[2], (TOKENS, D), 1.0, 6.0, ((0, 16),)),
        "buckets": touch_ends(jax.random.randint(key_list[3], (LEN, LEN), 0, BUCKETS), jax.random.fold_in(key_list[3], 1), 0, BUCKETS - 1).astype(jnp.int32),
        "gain_self": jnp.clip(1.0 + 0.1 * jax.random.normal(key_list[4], (D,), jnp.float32), 0.5, 1.5),
        "gain_cross": jnp.clip(1.0 + 0.1 * jax.random.normal(key_list[5], (D,), jnp.float32), 0.5, 1.5),
        "gain_ffn": jnp.clip(1.0 + 0.1 * jax.random.normal(key_list[6], (D,), jnp.float32), 0.5, 1.5),
        "bias_table": scatter_about(key_list[7], (BUCKETS, H), 1.0, 4.0, ((1, 2),), jnp.float32),
        "self_query": scatter_about(key_list[8], (D, H * HD), (16 * D) ** -0.5, 0.0546875, ((1, 2),)),
        "self_attention_key": scatter_about(key_list[9], (D, H * HD), D ** -0.5, 0.21875, ((1, 2),)),
        "self_value": scatter_about(key_list[10], (D, H * HD), D ** -0.5, 0.21875, ((1, 2),)),
        "self_out": scatter_about(key_list[11], (H * HD, D), (H * HD // 8) ** -0.5, 0.625, ((0, 2),)),
        "cross_query": scatter_about(key_list[12], (D, H * HD), (16 * D) ** -0.5, 0.0546875, ((1, 2),)),
        "cross_key": scatter_about(key_list[13], (D, H * HD), D ** -0.5, 0.21875, ((1, 2),)),
        "cross_value": scatter_about(key_list[14], (D, H * HD), D ** -0.5, 0.21875, ((1, 2),)),
        "cross_out": scatter_about(key_list[15], (H * HD, D), (H * HD // 8) ** -0.5, 0.625, ((0, 2),)),
        "ffn_gate": scatter_about(key_list[16], (D, FF), D ** -0.5, 0.21875, ((1, 2),)),
        "ffn_up": scatter_about(key_list[17], (D, FF), D ** -0.5, 0.21875, ((1, 2),)),
        "ffn_down": scatter_about(key_list[18], (FF, D), FF ** -0.5, 0.125, ((0, 2),)),
    }


epsilon = 1e-06
masked = -1e+30

def rms_apply(hidden, gain):
    scale = lax.rsqrt(lax.optimization_barrier(jnp.mean(hidden * hidden, axis=-1, keepdims=True)) + epsilon)
    return hidden * scale * gain

def glu_apply(gate, up):
    return jax.nn.gelu(gate, approximate=True) * up

def matmul(left, right):
    return jnp.dot(left, right, preferred_element_type=jnp.float32)

def rounded(values):
    return lax.optimization_barrier(values.astype(jnp.bfloat16)).astype(jnp.float32)

def heads_of(rows):
    return rows.reshape(rows.shape[0], H, HD).astype(jnp.float32)

def flatten(rows):
    return rows.reshape(rows.shape[0], H * HD).astype(jnp.bfloat16)

def attend(query, keys, values, extra):
    scores = jnp.einsum('qhd,khd->hqk', query, keys) + extra
    top = lax.optimization_barrier(jnp.max(scores, axis=-1, keepdims=True))
    lse = top + jnp.log(lax.optimization_barrier(jnp.sum(jnp.exp(scores - top), axis=-1, keepdims=True)))
    probs = jnp.exp(scores - lse)
    mixed = jnp.einsum('hqk,khd->qhd', rounded(probs), values)
    return (flatten(mixed), probs)

def attend_back(query, keys, values, probs, grad_mixed):
    grad_heads = heads_of(grad_mixed)
    dprob = jnp.einsum('qhd,khd->hqk', grad_heads, values)
    dscore = probs * (dprob - lax.optimization_barrier(jnp.sum(probs * dprob, axis=-1, keepdims=True)))
    score_low = rounded(dscore)
    dquery = jnp.einsum('hqk,khd->qhd', score_low, keys)
    dkeys = jnp.einsum('hqk,qhd->khd', score_low, query)
    dvalues = jnp.einsum('hqk,qhd->khd', rounded(probs), grad_heads)
    return (flatten(dquery), flatten(dkeys), flatten(dvalues), dscore)

def one_sequence(weights, extra, rows, enc_rows, grad_rows):
    gain_self, gain_cross, gain_ffn, sq, sk, sv, so, cq, ck, cv, co, fg, fu, fd = weights
    base = rows.astype(jnp.float32)
    first_normalized = rms_apply(base, gain_self).astype(jnp.bfloat16)
    q1 = matmul(first_normalized, sq).astype(jnp.bfloat16)
    k1 = matmul(first_normalized, sk).astype(jnp.bfloat16)
    v1 = matmul(first_normalized, sv).astype(jnp.bfloat16)
    mixed1, probs1 = attend(heads_of(q1), heads_of(k1), heads_of(v1), extra)
    first = base + matmul(mixed1, so)
    normed2 = rms_apply(first, gain_cross).astype(jnp.bfloat16)
    q2 = matmul(normed2, cq).astype(jnp.bfloat16)
    k2 = matmul(enc_rows, ck).astype(jnp.bfloat16)
    v2 = matmul(enc_rows, cv).astype(jnp.bfloat16)
    mixed2, probs2 = attend(heads_of(q2), heads_of(k2), heads_of(v2), jnp.float32(0.0))
    second = first + matmul(mixed2, co)
    normed3 = rms_apply(second, gain_ffn).astype(jnp.bfloat16)
    gate = matmul(normed3, fg)
    up = matmul(normed3, fu)
    hidden = glu_apply(gate, up).astype(jnp.bfloat16)
    output = (second + matmul(hidden, fd)).astype(jnp.bfloat16)
    grad_fd = matmul(hidden.T, grad_rows)
    grad_hidden = matmul(grad_rows, fd.T)
    _, pull = jax.vjp(glu_apply, gate, up)
    grad_gate, grad_up = pull(grad_hidden)
    grad_gate = grad_gate.astype(jnp.bfloat16)
    grad_up = grad_up.astype(jnp.bfloat16)
    grad_fg = matmul(normed3.T, grad_gate)
    feedforward_up_gradient = matmul(normed3.T, grad_up)
    grad_n3 = matmul(grad_gate, fg.T) + matmul(grad_up, fu.T)
    _, pull = jax.vjp(rms_apply, second, gain_ffn)
    back3, grad_gain_ffn = pull(grad_n3)
    grad_second = grad_rows.astype(jnp.float32) + back3
    second_low = grad_second.astype(jnp.bfloat16)
    grad_co = matmul(mixed2.T, second_low)
    grad_mixed2 = matmul(second_low, co.T).astype(jnp.bfloat16)
    dq2, dk2, dv2, unused = attend_back(heads_of(q2), heads_of(k2), heads_of(v2), probs2, grad_mixed2)
    grad_cq = matmul(normed2.T, dq2)
    grad_ck = matmul(enc_rows.T, dk2)
    grad_cv = matmul(enc_rows.T, dv2)
    grad_encoded = matmul(dk2, ck.T) + matmul(dv2, cv.T)
    second_norm_gradient = matmul(dq2, cq.T)
    _, pull = jax.vjp(rms_apply, first, gain_cross)
    back2, grad_gain_cross = pull(second_norm_gradient)
    grad_first = grad_second + back2
    first_low = grad_first.astype(jnp.bfloat16)
    grad_so = matmul(mixed1.T, first_low)
    grad_mixed1 = matmul(first_low, so.T).astype(jnp.bfloat16)
    dq1, self_key_delta, dv1, dscore1 = attend_back(heads_of(q1), heads_of(k1), heads_of(v1), probs1, grad_mixed1)
    grad_sq = matmul(first_normalized.T, dq1)
    grad_sk = matmul(first_normalized.T, self_key_delta)
    grad_sv = matmul(first_normalized.T, dv1)
    grad_n1 = matmul(dq1, sq.T) + matmul(self_key_delta, sk.T) + matmul(dv1, sv.T)
    _, pull = jax.vjp(rms_apply, base, gain_self)
    back1, grad_gain_self = pull(grad_n1)
    grad_input = grad_first + back1
    grads = (grad_gain_self, grad_gain_cross, grad_gain_ffn, grad_sq, grad_sk, grad_sv, grad_so, grad_cq, grad_ck, grad_cv, grad_co, grad_fg, feedforward_up_gradient, grad_fd)
    return (output, grad_input, grad_encoded, grads, dscore1)

def reference(inputs, encoded, cotangent, buckets, gain_self, gain_cross, gain_ffn, bias_table, self_query, self_attention_key, self_value, self_out, cross_query, cross_key, cross_value, cross_out, ffn_gate, ffn_up, ffn_down):
    weights = (gain_self, gain_cross, gain_ffn, self_query, self_attention_key, self_value, self_out, cross_query, cross_key, cross_value, cross_out, ffn_gate, ffn_up, ffn_down)
    table_hot = (buckets[:, :, None] == jnp.arange(BUCKETS, dtype=jnp.int32)[None, None, :]).astype(jnp.float32)
    bias = jnp.einsum('qkb,bh->hqk', table_hot, bias_table, precision=lax.Precision.HIGHEST)
    row_pos = jnp.arange(LEN, dtype=jnp.int32)[:, None]
    col_pos = jnp.arange(LEN, dtype=jnp.int32)[None, :]
    extra = jnp.where((col_pos <= row_pos)[None], bias, jnp.float32(masked))
    count = inputs.shape[0] // LEN
    rows3 = inputs.reshape(count, LEN, D)
    enc3 = encoded.reshape(count, ENC, D)
    grad3 = cotangent.reshape(count, LEN, D)

    def step(carry, items):
        output, grad_input, grad_encoded, grads, dscore = one_sequence(weights, extra, *items)
        carry = jax.tree.map(lambda left, right: left + right, carry, (grads, dscore))
        return (carry, (output, grad_input, grad_encoded))
    zeros = tuple((jnp.zeros(w.shape, jnp.float32) for w in weights))
    init = (zeros, jnp.zeros((H, LEN, LEN), jnp.float32))
    (grads, score_sum), (outputs, grad_inputs, grad_encs) = lax.scan(step, init, (rows3, enc3, grad3))
    table_grad = jnp.einsum('hqk,qkb->bh', score_sum, table_hot, precision=lax.Precision.HIGHEST)
    return (outputs.reshape(TOKENS, D), grad_inputs.reshape(TOKENS, D), grad_encs.reshape(ENC_TOKENS, D), grads[0], grads[1], grads[2], table_grad, grads[3], grads[4], grads[5], grads[6], grads[7], grads[8], grads[9], grads[10], grads[11], grads[12], grads[13])
```

```python
import jax
import jax.numpy as jnp
from jax import lax
from jax.sharding import PartitionSpec as P

HD = 64
LEN = 256
ENC = 256


epsilon = 1e-06
masked = -1e30


def rms_apply(hidden, gain):
    scale = lax.rsqrt(jnp.mean(hidden * hidden, axis=-1, keepdims=True) + epsilon)
    return hidden * scale * gain


def glu_apply(gate, up):
    return jax.nn.gelu(gate, approximate=True) * up


def matmul(left, right):
    return jnp.dot(left, right, preferred_element_type=jnp.float32)


def outer_product(left, right):
    return lax.dot_general(
        left, right, (((0,), (0,)), ((), ())), preferred_element_type=jnp.float32
    )


def back_product(left, weight):
    return lax.dot_general(
        left, weight, (((1,), (1,)), ((), ())), preferred_element_type=jnp.float32
    )


def to_heads(rows, length):
    return rows.reshape(rows.shape[0] // length, length, rows.shape[1] // HD, HD)


def to_rows(heads):
    return heads.reshape(heads.shape[0] * heads.shape[1], heads.shape[2] * HD)


def scores_of(query, keys, extra):
    return jnp.einsum("sqhd,skhd->shqk", query, keys, preferred_element_type=jnp.float32) + extra


def attend(query, keys, values, extra):
    scores = scores_of(query, keys, extra)
    top = jnp.max(scores, axis=-1, keepdims=True)
    lse = top + jnp.log(jnp.sum(jnp.exp(scores - top), axis=-1, keepdims=True))
    probs = jnp.exp(scores - lse).astype(jnp.bfloat16)
    mixed = jnp.einsum("shqk,skhd->sqhd", probs, values, preferred_element_type=jnp.float32)
    return (to_rows(mixed.astype(jnp.bfloat16)), lse)


def attend_back(query, keys, values, extra, lse, grad_mixed):
    probs = jnp.exp(scores_of(query, keys, extra) - lse)
    dprob = jnp.einsum("sqhd,skhd->shqk", grad_mixed, values, preferred_element_type=jnp.float32)
    dscore = probs * (dprob - jnp.sum(probs * dprob, axis=-1, keepdims=True))
    score_low = dscore.astype(jnp.bfloat16)
    dquery = jnp.einsum("shqk,skhd->sqhd", score_low, keys, preferred_element_type=jnp.float32)
    dkeys = jnp.einsum("shqk,sqhd->skhd", score_low, query, preferred_element_type=jnp.float32)
    dvalues = jnp.einsum(
        "shqk,sqhd->skhd",
        probs.astype(jnp.bfloat16),
        grad_mixed,
        preferred_element_type=jnp.float32,
    )
    return (
        to_rows(dquery.astype(jnp.bfloat16)),
        to_rows(dkeys.astype(jnp.bfloat16)),
        to_rows(dvalues.astype(jnp.bfloat16)),
        jnp.sum(dscore, axis=0),
    )


def flips(size, bit):
    return [(index, index ^ bit) for index in range(size)]


def swap_tensor(value):
    return lax.ppermute(value, "tensor", flips(lax.axis_size("tensor"), 1))


def sum_tensor(partial_rows):
    received = swap_tensor(partial_rows.astype(jnp.bfloat16))
    return partial_rows + received.astype(jnp.float32)


def scatter_tensor(partial_rows):
    halves = partial_rows.reshape(2, partial_rows.shape[0] // 2, partial_rows.shape[1])
    index = lax.axis_index("tensor")
    sent = lax.dynamic_index_in_dim(halves, 1 - index, 0, keepdims=False)
    kept = lax.dynamic_index_in_dim(halves, index, 0, keepdims=False)
    return kept + swap_tensor(sent.astype(jnp.bfloat16)).astype(jnp.float32)


def scatter_dp(partial_grad):
    size = lax.axis_size("dp")
    bits = size.bit_length() - 1
    index = lax.axis_index("dp")
    rows, columns = partial_grad.shape
    held = partial_grad.astype(jnp.bfloat16).reshape((2,) * bits + (rows // size, columns))
    for bit in range(bits):
        axis = bits - 1 - bit
        side = (index >> bit) & 1
        sent = lax.dynamic_index_in_dim(held, 1 - side, axis, keepdims=False)
        kept = lax.dynamic_index_in_dim(held, side, axis, keepdims=False)
        received = lax.ppermute(sent, "dp", flips(size, 1 << bit))
        held = kept.astype(jnp.float32) + received.astype(jnp.float32)
        if bit < bits - 1:
            held = held.astype(jnp.bfloat16)
    return held


def sum_small(gains, table):
    size = lax.axis_size("dp")
    packed = jnp.concatenate([gains.reshape(-1), table.reshape(-1)])
    bit = 1
    while bit < size:
        packed = packed + lax.ppermute(packed, "dp", flips(size, bit))
        bit *= 2
    gains = packed[: gains.size].reshape(gains.shape)
    gains = gains + swap_tensor(gains)
    return gains, packed[gains.size :].reshape(table.shape)


def body(
    inputs,
    encoded,
    cotangent,
    buckets,
    gain_self,
    gain_cross,
    gain_ffn,
    bias_table,
    self_query,
    self_attention_key,
    self_value,
    self_out,
    cross_query,
    cross_key,
    cross_value,
    cross_out,
    ffn_gate,
    ffn_up,
    ffn_down,
):
    groups = lax.axis_size("tensor")
    share = inputs.shape[0] // groups
    offset = lax.axis_index("tensor") * share

    def own_rows(rows):
        return lax.dynamic_slice_in_dim(rows, offset, share, 0)

    table_hot = (
        buckets[:, :, None] == jnp.arange(bias_table.shape[0], dtype=jnp.int32)[None, None, :]
    ).astype(jnp.float32)
    bias = jnp.einsum("qkb,bh->hqk", table_hot, bias_table, precision=lax.Precision.HIGHEST)
    row_pos = jnp.arange(LEN, dtype=jnp.int32)[:, None]
    col_pos = jnp.arange(LEN, dtype=jnp.int32)[None, :]
    extra = jnp.where((col_pos <= row_pos)[None], bias, jnp.float32(masked))[None]
    base = inputs.astype(jnp.float32)
    first_normalized = rms_apply(base, gain_self).astype(jnp.bfloat16)
    q1 = to_heads(matmul(first_normalized, self_query).astype(jnp.bfloat16), LEN)
    k1 = to_heads(matmul(first_normalized, self_attention_key).astype(jnp.bfloat16), LEN)
    v1 = to_heads(matmul(first_normalized, self_value).astype(jnp.bfloat16), LEN)
    mixed1, lse1 = attend(q1, k1, v1, extra)
    first = base + sum_tensor(matmul(mixed1, self_out))
    normed2 = rms_apply(first, gain_cross).astype(jnp.bfloat16)
    q2 = to_heads(matmul(normed2, cross_query).astype(jnp.bfloat16), LEN)
    k2 = to_heads(matmul(encoded, cross_key).astype(jnp.bfloat16), ENC)
    v2 = to_heads(matmul(encoded, cross_value).astype(jnp.bfloat16), ENC)
    mixed2, lse2 = attend(q2, k2, v2, jnp.float32(0.0))
    second = first + sum_tensor(matmul(mixed2, cross_out))
    normed3 = rms_apply(second, gain_ffn).astype(jnp.bfloat16)
    gate = matmul(normed3, ffn_gate)
    up = matmul(normed3, ffn_up)
    hidden = glu_apply(gate, up).astype(jnp.bfloat16)
    grad_hidden = back_product(cotangent, ffn_down)
    unused, pull = jax.vjp(glu_apply, gate, up)
    grad_gate, grad_up = pull(grad_hidden)
    grad_gate = grad_gate.astype(jnp.bfloat16)
    grad_up = grad_up.astype(jnp.bfloat16)
    grad_n3 = sum_tensor(back_product(grad_gate, ffn_gate) + back_product(grad_up, ffn_up))
    ffn_parts = jnp.concatenate(
        [
            outer_product(cotangent, hidden).astype(jnp.bfloat16),
            outer_product(normed3, grad_gate).astype(jnp.bfloat16),
            outer_product(normed3, grad_up).astype(jnp.bfloat16),
        ],
        axis=1,
    )
    ffn_total = scatter_dp(ffn_parts)
    output = (own_rows(second) + scatter_tensor(matmul(hidden, ffn_down))).astype(jnp.bfloat16)
    unused, pull = jax.vjp(rms_apply, second, gain_ffn)
    back3, unused_gain = pull(grad_n3)
    unused, pull_gain = jax.vjp(lambda gain: rms_apply(own_rows(second), gain), gain_ffn)
    (grad_gain_ffn,) = pull_gain(own_rows(grad_n3))
    grad_second = cotangent.astype(jnp.float32) + back3
    second_low = grad_second.astype(jnp.bfloat16)
    grad_mixed2 = to_heads(back_product(second_low, cross_out).astype(jnp.bfloat16), LEN)
    dq2, dk2, dv2, unused_sum = attend_back(q2, k2, v2, jnp.float32(0.0), lse2, grad_mixed2)
    grad_n2 = sum_tensor(back_product(dq2, cross_query))
    cross_parts = jnp.concatenate(
        [
            outer_product(second_low, mixed2).astype(jnp.bfloat16),
            outer_product(normed2, dq2).astype(jnp.bfloat16),
            outer_product(encoded, dk2).astype(jnp.bfloat16),
            outer_product(encoded, dv2).astype(jnp.bfloat16),
        ],
        axis=1,
    )
    cross_total = scatter_dp(cross_parts)
    grad_encoded = scatter_tensor(back_product(dk2, cross_key) + back_product(dv2, cross_value))
    unused, pull = jax.vjp(rms_apply, first, gain_cross)
    back2, unused_gain = pull(grad_n2)
    unused, pull_gain = jax.vjp(lambda gain: rms_apply(own_rows(first), gain), gain_cross)
    (grad_gain_cross,) = pull_gain(own_rows(grad_n2))
    grad_first = grad_second + back2
    first_low = grad_first.astype(jnp.bfloat16)
    grad_mixed1 = to_heads(back_product(first_low, self_out).astype(jnp.bfloat16), LEN)
    dq1, dk1, dv1, score_sum = attend_back(q1, k1, v1, extra, lse1, grad_mixed1)
    self_parts = jnp.concatenate(
        [
            outer_product(first_low, mixed1).astype(jnp.bfloat16),
            outer_product(first_normalized, dq1).astype(jnp.bfloat16),
            outer_product(first_normalized, dk1).astype(jnp.bfloat16),
            outer_product(first_normalized, dv1).astype(jnp.bfloat16),
        ],
        axis=1,
    )
    self_total = scatter_dp(self_parts)
    grad_n1 = scatter_tensor(
        back_product(dq1, self_query)
        + back_product(dk1, self_attention_key)
        + back_product(dv1, self_value)
    )
    unused, pull = jax.vjp(rms_apply, own_rows(base), gain_self)
    back1, grad_gain_self = pull(grad_n1)
    input_grad = own_rows(grad_first) + back1
    grad_table = jnp.einsum("hqk,qkb->bh", score_sum, table_hot, precision=lax.Precision.HIGHEST)
    gains, table_total = sum_small(
        jnp.stack([grad_gain_self, grad_gain_cross, grad_gain_ffn]), grad_table
    )
    units = ffn_gate.shape[1]
    heads = self_query.shape[1]
    return (
        output,
        input_grad,
        grad_encoded,
        gains[0],
        gains[1],
        gains[2],
        table_total,
        self_total[:, heads : 2 * heads],
        self_total[:, 2 * heads : 3 * heads],
        self_total[:, 3 * heads :],
        self_total[:, :heads].T,
        cross_total[:, heads : 2 * heads],
        cross_total[:, 2 * heads : 3 * heads],
        cross_total[:, 3 * heads :],
        cross_total[:, :heads].T,
        ffn_total[:, units : 2 * units],
        ffn_total[:, 2 * units :],
        ffn_total[:, :units].T,
    )


def solution(mesh):
    in_specs = (
        P("dp", None),
        P("dp", None),
        P("dp", None),
        P(),
        P(),
        P(),
        P(),
        P(None, "tensor"),
        P(None, "tensor"),
        P(None, "tensor"),
        P(None, "tensor"),
        P("tensor", None),
        P(None, "tensor"),
        P(None, "tensor"),
        P(None, "tensor"),
        P("tensor", None),
        P(None, "tensor"),
        P(None, "tensor"),
        P("tensor", None),
    )
    out_specs = (
        P(("dp", "tensor"), None),
        P(("dp", "tensor"), None),
        P(("dp", "tensor"), None),
        P(),
        P(),
        P(),
        P(None, "tensor"),
        P("dp", "tensor"),
        P("dp", "tensor"),
        P("dp", "tensor"),
        P("tensor", "dp"),
        P("dp", "tensor"),
        P("dp", "tensor"),
        P("dp", "tensor"),
        P("tensor", "dp"),
        P("dp", "tensor"),
        P("dp", "tensor"),
        P("tensor", "dp"),
    )
    return jax.shard_map(body, mesh=mesh, in_specs=in_specs, out_specs=out_specs, check_vma=False)
```

```python
import functools

import jax
import jax.numpy as jnp
from jax import lax
from jax.experimental import pallas as pl
from jax.experimental.pallas import tpu as pltpu
from jax.sharding import PartitionSpec as P


HD = 64
LEN = 256
LANES = 128
PIECE = 256


epsilon = 1e-06
masked = -1e30
bend = 0.044715
slope = 0.7978845608028654

f32 = jnp.float32
bf16 = jnp.bfloat16


def dot(left, right):
    return jnp.dot(left, right, preferred_element_type=f32)


def dot_back(left, weight):
    return lax.dot_general(left, weight, (((1,), (1,)), ((), ())), preferred_element_type=f32)


def dot_outer(left, right):
    return lax.dot_general(left, right, (((0,), (0,)), ((), ())), preferred_element_type=f32)


def rms(hidden, gain):
    scale = lax.rsqrt(jnp.mean(hidden * hidden, axis=-1, keepdims=True) + epsilon)
    return hidden * scale * gain


def rms_back(hidden, gain, grad):
    scale = lax.rsqrt(jnp.mean(hidden * hidden, axis=-1, keepdims=True) + epsilon)
    unit = hidden * scale
    pulled = grad * gain
    along = jnp.mean(pulled * unit, axis=-1, keepdims=True)
    return scale * (pulled - unit * along), grad * unit


def pair_mask(rows, side):
    lane = lax.broadcasted_iota(jnp.int32, (rows, LANES), 1)
    return (lane >= HD) == (side == 1)


def keep_side(rows, side):
    return jnp.where(pair_mask(rows.shape[0], side), rows, jnp.zeros_like(rows))


def softmax(scores):
    top = jnp.max(scores, axis=-1, keepdims=True)
    weights = jnp.exp(scores - top)
    return weights * (1.0 / jnp.sum(weights, axis=-1, keepdims=True))


def heads_forward(query, keys, values, extra_of, probs_out, mixed_out):
    for pair in range(query.shape[1] // LANES):
        lanes = slice(pair * LANES, (pair + 1) * LANES)
        probs, sides = [], []
        for side in range(2):
            scores = dot_back(keep_side(query[:, lanes], side), keys[:, lanes])
            head_probs = softmax(extra_of(scores, 2 * pair + side))
            probs_out[2 * pair + side] = head_probs
            probs.append(head_probs.astype(bf16))
            sides.append(keep_side(values[:, lanes], side))
        mixed = dot(jnp.concatenate(probs, axis=1), jnp.concatenate(sides, axis=0))
        mixed_out[:, lanes] = mixed.astype(bf16)


def heads_backward(query, keys, values, probs_in, grad_mixed, outs, dscore_out):
    dquery_out, dkeys_out, dvalues_out = outs
    for pair in range(query.shape[1] // LANES):
        lanes = slice(pair * LANES, (pair + 1) * LANES)
        scores_low, key_sides, query_sides, probs_low, grad_sides = [], [], [], [], []
        for side in range(2):
            probs = probs_in[2 * pair + side]
            grad_side = keep_side(grad_mixed[:, lanes], side)
            dprob = dot_back(grad_side, values[:, lanes])
            dscore = probs * (dprob - jnp.sum(probs * dprob, axis=-1, keepdims=True))
            if dscore_out is not None:
                dscore_out[2 * pair + side] = dscore
            scores_low.append(dscore.astype(bf16))
            probs_low.append(probs.astype(bf16))
            key_sides.append(keep_side(keys[:, lanes], side))
            query_sides.append(keep_side(query[:, lanes], side))
            grad_sides.append(grad_side)
        dquery = dot(jnp.concatenate(scores_low, axis=1), jnp.concatenate(key_sides, axis=0))
        dquery_out[:, lanes] = dquery.astype(bf16)
        dkeys = dot_outer(
            jnp.concatenate(scores_low, axis=0), jnp.concatenate(query_sides, axis=0)
        )
        dkeys_out[:, lanes] = dkeys.astype(bf16)
        dvalues = dot_outer(
            jnp.concatenate(probs_low, axis=0), jnp.concatenate(grad_sides, axis=0)
        )
        dvalues_out[:, lanes] = dvalues.astype(bf16)


def own_part(terms):
    share = terms.shape[0] // 2
    row = lax.broadcasted_iota(jnp.int32, terms.shape, 0)
    mine = (row >= share) == (lax.axis_index("tensor") == 1)
    return jnp.sum(jnp.where(mine, terms, 0.0), axis=0, keepdims=True)


def own_rows_of(ref, other=False):
    share = ref.shape[0] // 2
    index = lax.axis_index("tensor")
    index = 1 - index if other else index
    return ref[pl.ds(pl.multiple_of(index * share, share), share), :]


def self_forward(
    inputs, gain, sq, sk, sv, so, buckets, table,
    normed_out, q_out, k_out, v_out, probs_out, mixed_out, kept_out, sent_out,
):
    normed = rms(inputs[...].astype(f32), gain[...]).astype(bf16)
    normed_out[...] = normed
    q_out[...] = dot(normed, sq[...]).astype(bf16)
    k_out[...] = dot(normed, sk[...]).astype(bf16)
    v_out[...] = dot(normed, sv[...]).astype(bf16)
    count = table.shape[1]
    row = lax.broadcasted_iota(jnp.int32, (count, LANES), 0)
    lane = lax.broadcasted_iota(jnp.int32, (count, LANES), 1)
    by_lane = jnp.dot(
        table[...],
        (row == lane).astype(f32),
        preferred_element_type=f32,
        precision=lax.Precision.HIGHEST,
    )
    length = inputs.shape[0]
    causal = lax.broadcasted_iota(jnp.int32, (length, length), 1) <= lax.broadcasted_iota(
        jnp.int32, (length, length), 0
    )

    def extra_of(scores, head):
        values = jnp.broadcast_to(by_lane[head : head + 1, :], (length, LANES))
        bias = jnp.concatenate(
            [
                jnp.take_along_axis(
                    values,
                    buckets[:, at : at + LANES],
                    axis=1,
                    mode="promise_in_bounds",
                )
                for at in range(0, length, LANES)
            ],
            axis=1,
        )
        return jnp.where(causal, scores + bias, masked)

    heads_forward(q_out, k_out, v_out, extra_of, probs_out, mixed_out)
    part = dot(mixed_out[...], so[...])
    kept_out[...] = part
    sent_out[...] = part.astype(bf16)


def cross_keys(encoded, ck, cv, k_out, v_out):
    k_out[...] = dot(encoded[...], ck[...]).astype(bf16)
    v_out[...] = dot(encoded[...], cv[...]).astype(bf16)


def cross_forward(
    inputs, kept, got, gain, cq, keys, values, co,
    first_out, normed_out, q_out, probs_out, mixed_out, kept_out, sent_out,
):
    first = inputs[...].astype(f32) + (kept[...] + got[...].astype(f32))
    first_out[...] = first
    normed = rms(first, gain[...]).astype(bf16)
    normed_out[...] = normed
    q_out[...] = dot(normed, cq[...]).astype(bf16)
    heads_forward(q_out, keys, values, lambda scores, head: scores, probs_out, mixed_out)
    part = dot(mixed_out[...], co[...])
    kept_out[...] = part
    sent_out[...] = part.astype(bf16)


def hidden_back(cotangent, fd, dhidden_out):
    dhidden_out[...] = dot_back(cotangent[...], fd[...])


def ffn_both(
    first, kept, got, gain, fg, fu, dhidden,
    second_out, normed_out, hidden_out, dgate_out, dup_out, kept_out, sent_out,
):
    second = first[...] + (kept[...] + got[...].astype(f32))
    second_out[...] = second
    normed = rms(second, gain[...]).astype(bf16)
    normed_out[...] = normed
    total = jnp.zeros(second.shape, f32)
    for at in range(0, fg.shape[1], PIECE):
        units = slice(at, at + PIECE)
        gate = dot(normed, fg[:, units])
        up = dot(normed, fu[:, units])
        square = gate * gate
        bent = jnp.tanh(slope * (gate + bend * (square * gate)))
        half = 0.5 * (1.0 + bent)
        gelu = gate * half
        hidden_out[:, units] = (gelu * up).astype(bf16)
        rise = half + 0.5 * gate * (1.0 - bent * bent) * (slope * (1.0 + 3.0 * bend * square))
        grad = dhidden[:, units]
        dgate = (grad * up * rise).astype(bf16)
        dup = (grad * gelu).astype(bf16)
        dgate_out[:, units] = dgate
        dup_out[:, units] = dup
        total = total + (dot_back(dgate, fg[:, units]) + dot_back(dup, fu[:, units]))
    kept_out[...] = total
    sent_out[...] = total.astype(bf16)


def ffn_output(hidden, fd, second, kept_out, sent_out, total):
    total[...] = dot(hidden[...], fd[...])
    kept_out[...] = own_rows_of(second) + own_rows_of(total)
    sent_out[...] = own_rows_of(total, True).astype(bf16)


def cross_backward(
    second, cotangent, kept, got, gain, co, cq, query, keys, values, probs,
    dsecond_out, low_out, dq_out, dk_out, dv_out, kept_out, sent_out, gain_out,
):
    back, terms = rms_back(second[...], gain[...], kept[...] + got[...].astype(f32))
    gain_out[...] = own_part(terms)
    dsecond = cotangent[...].astype(f32) + back
    dsecond_out[...] = dsecond
    low = dsecond.astype(bf16)
    low_out[...] = low
    grad_mixed = dot_back(low, co[...]).astype(bf16)
    heads_backward(query, keys, values, probs, grad_mixed, (dq_out, dk_out, dv_out), None)
    part = dot_back(dq_out[...], cq[...])
    kept_out[...] = part
    sent_out[...] = part.astype(bf16)


def encoded_back(dk, dv, ck, cv, kept_out, sent_out, total):
    total[...] = dot_back(dk[...], ck[...]) + dot_back(dv[...], cv[...])
    kept_out[...] = own_rows_of(total)
    sent_out[...] = own_rows_of(total, True).astype(bf16)


def self_backward(
    first, dsecond, kept, got, gain, so, sq, sk, sv, query, keys, values, probs,
    dfirst_out, low_out, dq_out, dk_out, dv_out, dscore_out, kept_out, sent_out, gain_out, total,
):
    back, terms = rms_back(first[...], gain[...], kept[...] + got[...].astype(f32))
    gain_out[...] = own_part(terms)
    dfirst = dsecond[...] + back
    total[...] = dfirst
    dfirst_out[...] = own_rows_of(total)
    low = dfirst.astype(bf16)
    low_out[...] = low
    grad_mixed = dot_back(low, so[...]).astype(bf16)
    heads_backward(query, keys, values, probs, grad_mixed, (dq_out, dk_out, dv_out), dscore_out)
    total[...] = (
        dot_back(dq_out[...], sq[...]) + dot_back(dk_out[...], sk[...])
    ) + dot_back(dv_out[...], sv[...])
    kept_out[...] = own_rows_of(total)
    sent_out[...] = own_rows_of(total, True).astype(bf16)


def last_back(inputs, dfirst, kept, got, gain, grad_out, gain_out):
    own = own_rows_of(inputs).astype(f32)
    back, terms = rms_back(own, gain[...], kept[...] + got[...].astype(f32))
    gain_out[...] = jnp.sum(terms, axis=0, keepdims=True)
    grad_out[...] = dfirst[...] + back


def weight_grads(places, block, *refs):
    inputs, (kept_out, sent_out, product) = refs[:-3], refs[-3:]
    side = lax.axis_index("dp") & 1
    column = 0
    turned = {}
    for left, right in places:
        if left not in turned:
            turned[left] = inputs[left][...].T
        width = inputs[right].shape[1]
        for at in range(0, width, PIECE):
            span = min(PIECE, width - at)
            product[:, :span] = dot(turned[left], inputs[right][:, at : at + span])
            columns = slice(column, column + span)
            for pair in range(product.shape[0] // (2 * block)):
                rows = slice(pair * block, (pair + 1) * block)
                kept_at = pl.multiple_of((2 * pair + side) * block, 16)
                sent_at = pl.multiple_of((2 * pair + 1 - side) * block, 16)
                kept_out[rows, columns] = product[pl.ds(kept_at, block), :span].astype(bf16)
                sent_out[rows, columns] = product[pl.ds(sent_at, block), :span].astype(bf16)
            column += span


def halve(block, bit, kept, got, kept_out, sent_out):
    side = (lax.axis_index("dp") >> bit) & 1
    for pair in range(kept.shape[0] // (2 * block)):
        rows = slice(pair * block, (pair + 1) * block)
        for place, out in ((side, kept_out), (1 - side, sent_out)):
            at = pl.ds(pl.multiple_of((2 * pair + place) * block, 16), block)
            out[rows, :] = (kept[at, :].astype(f32) + got[at, :].astype(f32)).astype(bf16)


def finish(kept, got, *outs):
    column = 0
    for out in outs:
        columns = slice(column, column + out.shape[1])
        out[...] = kept[:, columns].astype(f32) + got[:, columns].astype(f32)
        column += out.shape[1]


def table_grad(dscore, buckets, out, lines):
    count = out.shape[1]

    def add_bucket(bucket, carry):
        hit = buckets[...] == bucket
        for head in range(dscore.shape[0]):
            chosen = jnp.where(hit, dscore[head], 0.0)
            lines[head, pl.ds(bucket, 1), :] = jnp.sum(chosen, axis=0, keepdims=True)
        return carry

    lax.fori_loop(0, count, add_bucket, 0)
    out[...] = jnp.sum(lines[...], axis=-1)


def shape(dims, kind):
    return jax.ShapeDtypeStruct(dims, kind)


def call(kernel, outs, args, flops, scratch=()):
    moved = sum(item.size * item.dtype.itemsize for item in (*outs, *args))
    return pl.pallas_call(
        kernel,
        out_shape=tuple(outs),
        scratch_shapes=list(scratch),
        compiler_params=pltpu.CompilerParams(vmem_limit_bytes=24 << 20),
        cost_estimate=pl.CostEstimate(flops=flops, bytes_accessed=moved, transcendentals=0),
    )(*args)


def flips(size, bit):
    return [(index, index ^ bit) for index in range(size)]


def swap_tensor(value):
    return lax.ppermute(value, "tensor", flips(lax.axis_size("tensor"), 1))


def grads_of(arrays, places, block):
    rows = arrays[places[0][0]].shape[1]
    width = sum(arrays[right].shape[1] for _, right in places)
    if block % 16 == 0:
        flops = 2 * LEN * rows * width
        half = shape((rows // 2, width), bf16)
        return call(
            functools.partial(weight_grads, places, block),
            (half, half),
            arrays,
            flops,
            [pltpu.VMEM((rows, PIECE), f32)],
        )
    parts = [dot_outer(arrays[left], arrays[right]).astype(bf16) for left, right in places]
    whole = jnp.concatenate(parts, axis=1).reshape(-1, 2, block, width)
    side = lax.axis_index("dp") & 1
    kept = lax.dynamic_index_in_dim(whole, side, 1, keepdims=False)
    sent = lax.dynamic_index_in_dim(whole, 1 - side, 1, keepdims=False)
    return kept.reshape(-1, width), sent.reshape(-1, width)


def scatter_dp(kept, sent, widths):
    size = lax.axis_size("dp")
    bits = size.bit_length() - 1
    index = lax.axis_index("dp")
    columns = kept.shape[1]
    block = kept.shape[0] * 2 // size
    for bit in range(bits):
        received = lax.ppermute(sent, "dp", flips(size, 1 << bit))
        if bit == bits - 1:
            outs = [shape((block, width), f32) for width in widths]
            return call(finish, outs, (kept, received), 0)
        if block % 16 == 0:
            half = shape((kept.shape[0] // 2, columns), bf16)
            kept, sent = call(
                functools.partial(halve, block, bit + 1), (half, half), (kept, received), 0
            )
        else:
            held = (kept.astype(f32) + received.astype(f32)).astype(bf16)
            held = held.reshape(-1, 2, block, columns)
            side = (index >> (bit + 1)) & 1
            kept = lax.dynamic_index_in_dim(held, side, 1, keepdims=False)
            sent = lax.dynamic_index_in_dim(held, 1 - side, 1, keepdims=False)
            kept, sent = kept.reshape(-1, columns), sent.reshape(-1, columns)


def sum_small(gains, table):
    size = lax.axis_size("dp")
    packed = jnp.concatenate([gains.reshape(-1), table.reshape(-1)])
    bit = 1
    while bit < size:
        packed = packed + lax.ppermute(packed, "dp", flips(size, bit))
        bit *= 2
    gains = packed[: gains.size].reshape(gains.shape)
    gains = gains + swap_tensor(gains)
    return gains, packed[gains.size :].reshape(table.shape)


def body(
    inputs,
    encoded,
    cotangent,
    buckets,
    gain_self,
    gain_cross,
    gain_ffn,
    bias_table,
    self_query,
    self_attention_key,
    self_value,
    self_out,
    cross_query,
    cross_key,
    cross_value,
    cross_out,
    ffn_gate,
    ffn_up,
    ffn_down,
):
    rows, width = inputs.shape
    assert rows == LEN and encoded.shape[0] == LEN and lax.axis_size("tensor") == 2
    heads_width = self_query.shape[1]
    heads = heads_width // HD
    units = ffn_gate.shape[1]
    assert heads_width % LANES == 0 and units % PIECE == 0
    block = width // lax.axis_size("dp")
    share = rows // 2
    gain_self = gain_self.reshape(1, width)
    gain_cross = gain_cross.reshape(1, width)
    gain_ffn = gain_ffn.reshape(1, width)
    full32, full16 = shape((rows, width), f32), shape((rows, width), bf16)
    half32, half16 = shape((share, width), f32), shape((share, width), bf16)
    mix16 = shape((rows, heads_width), bf16)
    hid16 = shape((rows, units), bf16)
    probs32 = shape((heads, rows, rows), f32)
    line = shape((1, width), f32)
    scratch = [pltpu.VMEM((rows, width), f32)]
    one = 2 * rows * width * heads_width
    wide = 2 * rows * width * units

    normed1, q1, k1, v1, probs1, mixed1, kept1, sent1 = call(
        self_forward,
        (full16, mix16, mix16, mix16, probs32, mix16, full32, full16),
        (inputs, gain_self, self_query, self_attention_key, self_value, self_out, buckets, bias_table.T),
        6 * one,
    )
    got1 = swap_tensor(sent1)
    k2, v2 = call(cross_keys, (mix16, mix16), (encoded, cross_key, cross_value), 2 * one)
    first, normed2, q2, probs2, mixed2, kept2, sent2 = call(
        cross_forward,
        (full32, full16, mix16, probs32, mix16, full32, full16),
        (inputs, kept1, got1, gain_cross, cross_query, k2, v2, cross_out),
        4 * one,
    )
    got2 = swap_tensor(sent2)
    (dhidden,) = call(hidden_back, (shape((rows, units), f32),), (cotangent, ffn_down), wide)
    second, normed3, hidden, dgate, dup, kept4, sent4 = call(
        ffn_both,
        (full32, full16, hid16, hid16, hid16, full32, full16),
        (first, kept2, got2, gain_ffn, ffn_gate, ffn_up, dhidden),
        4 * wide,
    )
    got4 = swap_tensor(sent4)
    ffn_kept, ffn_sent = grads_of(
        (cotangent, hidden, normed3, dgate, dup), ((0, 1), (2, 3), (2, 4)), block
    )
    kept3, sent3 = call(ffn_output, (half32, half16), (hidden, ffn_down, second), wide, scratch)
    dsecond, low2, dq2, dk2, dv2, kept5, sent5, gain_two = call(
        cross_backward,
        (full32, full16, mix16, mix16, mix16, full32, full16, line),
        (second, cotangent, kept4, got4, gain_ffn, cross_out, cross_query, q2, k2, v2, probs2),
        5 * one,
    )
    got3 = swap_tensor(sent3)
    output = (kept3 + got3.astype(f32)).astype(bf16)
    got5 = swap_tensor(sent5)
    cross_kept, cross_sent = grads_of(
        (low2, mixed2, normed2, dq2, encoded, dk2, dv2), ((0, 1), (2, 3), (4, 5), (4, 6)), block
    )
    kept7, sent7 = call(
        encoded_back, (half32, half16), (dk2, dv2, cross_key, cross_value), 2 * one, scratch
    )
    dfirst, low1, dq1, dk1, dv1, dscore1, kept6, sent6, gain_one = call(
        self_backward,
        (half32, full16, mix16, mix16, mix16, probs32, half32, half16, line),
        (
            first, dsecond, kept5, got5, gain_cross, self_out, self_query,
            self_attention_key, self_value, q1, k1, v1, probs1,
        ),
        7 * one,
        scratch,
    )
    got7 = swap_tensor(sent7)
    grad_encoded = kept7 + got7.astype(f32)
    self_kept, self_sent = grads_of(
        (low1, mixed1, normed1, dq1, dk1, dv1), ((0, 1), (2, 3), (2, 4), (2, 5)), block
    )
    got6 = swap_tensor(sent6)
    input_grad, gain_zero = call(
        last_back, (half32, line), (inputs, dfirst, kept6, got6, gain_self), 0
    )
    table_hits = call(
        table_grad,
        (shape((heads, bias_table.shape[0]), f32),),
        (dscore1, buckets),
        0,
        [pltpu.VMEM((heads, bias_table.shape[0], rows), f32)],
    )[0]
    wide_parts = scatter_dp(ffn_kept, ffn_sent, (units,) * 3)
    cross_parts = scatter_dp(cross_kept, cross_sent, (heads_width,) * 4)
    self_parts = scatter_dp(self_kept, self_sent, (heads_width,) * 4)
    gains, table_total = sum_small(
        jnp.concatenate([gain_zero, gain_one, gain_two], axis=0), table_hits
    )
    return (
        output,
        input_grad,
        grad_encoded,
        gains[0],
        gains[1],
        gains[2],
        table_total.T,
        self_parts[1],
        self_parts[2],
        self_parts[3],
        self_parts[0].T,
        cross_parts[1],
        cross_parts[2],
        cross_parts[3],
        cross_parts[0].T,
        wide_parts[1],
        wide_parts[2],
        wide_parts[0].T,
    )


def solution(mesh):
    in_specs = (
        P("dp", None),
        P("dp", None),
        P("dp", None),
        P(),
        P(),
        P(),
        P(),
        P(None, "tensor"),
        P(None, "tensor"),
        P(None, "tensor"),
        P(None, "tensor"),
        P("tensor", None),
        P(None, "tensor"),
        P(None, "tensor"),
        P(None, "tensor"),
        P("tensor", None),
        P(None, "tensor"),
        P(None, "tensor"),
        P("tensor", None),
    )
    out_specs = (
        P(("dp", "tensor"), None),
        P(("dp", "tensor"), None),
        P(("dp", "tensor"), None),
        P(),
        P(),
        P(),
        P(None, "tensor"),
        P("dp", "tensor"),
        P("dp", "tensor"),
        P("dp", "tensor"),
        P("tensor", "dp"),
        P("dp", "tensor"),
        P("dp", "tensor"),
        P("dp", "tensor"),
        P("tensor", "dp"),
        P("dp", "tensor"),
        P("dp", "tensor"),
        P("tensor", "dp"),
    )
    return jax.shard_map(body, mesh=mesh, in_specs=in_specs, out_specs=out_specs, check_vma=False)
```
